128 devices in a mesh: freq: 8 (over x, z_hi), blk: 16 (over y, z_lo, core).
Axes of the slice: x: 4, y: 4, z: 4 (z_hi: 2, z_lo: 2; z = z_hi * 2 + z_lo), core: 2. Of those that a mesh axis runs over, the one named last changes fastest.
Arguments:
- reflection: bfloat16 [16, 2, 6144, 6144], P('freq', None, 'blk'), as said below
- direct_focus: bfloat16 [32, 1024, 6144], P('freq', None, 'blk'), may hold values from -6 to 6
- onset: int32 [32, 6144], P('freq', 'blk'), may hold values from 64 to 81
Outputs:
- focused: bfloat16 [32, 1024, 6144], P('freq', None, 'blk')
The draws below stay inside these ranges and needn't reach their ends.
Inputs may be any that keep to these rules, and one draw needn't show every extreme that they name: For every frequency, the real and the imaginary matrix of reflection are each symmetric (source-receiver reciprocity).
All inputs are finite; a program needn't handle non-finite values.
Results may differ from the reference program's by a relative error of at most 0.02.
Values may be sent and summed in bfloat16 or wider, within the bound.
No kernel may reach another device: no remote copies, remote signals or barrier semaphores. Data moves between devices by JAX's collectives and lax.ppermute only.
A program may use at most 128 MiB of HBM per device.

```python
import math
import jax
import jax.numpy as jnp
from jax import lax

FOC = 32
NT = 1024
ITERS = 3
ORDER = 6144
NF = 16


def draw_reflection(key, part):

    def single(index):
        subkey = jax.random.fold_in(key, index)
        shape = (2, ORDER, ORDER)
        base = jax.random.normal(subkey, shape, jnp.float32)
        symmetric = (base + jnp.swapaxes(base, 1, 2)) * (4.0 * math.sqrt(0.5) * (2.0 * ORDER) ** (-0.5))
        return symmetric.astype(jnp.bfloat16)
    return lax.map(single, jnp.arange(NF, dtype=jnp.int32))


def set_ends(drawn, rng, smallest, high):
    dims = drawn.shape
    place = [jax.random.randint(jax.random.fold_in(rng, axis), (), 0, dims[axis]) for axis in range(len(dims))]
    drawn = drawn.at[tuple(place)].set(smallest)
    longest = dims.index(max(dims))
    place[longest] = (place[longest] + 1) % dims[longest]
    return drawn.at[tuple(place)].set(high)


def block_levels(own_key, dims, cuts, least, high):
    def one(axis_at, shards_of):
        draws = jax.random.uniform(jax.random.fold_in(jax.random.fold_in(own_key, 6), axis_at), (shards_of,), jnp.float32, least / len(cuts), high / len(cuts))
        return jnp.repeat(jnp.exp(draws), dims[axis_at] // shards_of).reshape((-1,) + (1,) * (len(dims) - axis_at - 1))

    loudness = one(*cuts[0])
    for cut in cuts[1:]:
        loudness = loudness * one(*cut)
    return loudness


def centred(own_key, dims, deviation, limit, shards=(), held_as=jnp.bfloat16):
    factor_of = block_levels(own_key, dims, shards, -0.22, 0.18) if shards else 1.0
    values = jax.random.normal(own_key, dims, jnp.float32) * deviation * factor_of
    return jnp.minimum(jnp.maximum(values, -limit), limit).astype(held_as)


def setup_inputs(seed: int = 0) -> dict:
    key_list = jax.random.split(jax.random.key(seed), 4)
    return {
        "reflection": draw_reflection(jax.random.fold_in(key_list[3], 71), 0),
        "direct_focus": centred(key_list[1], (FOC, NT, ORDER), 1.0, 6.0, ((0, 8), (2, 16))),
        "onset": set_ends(jax.random.randint(key_list[2], (FOC, ORDER), NT // 16, NT // 16 + NT // 64 + 2), jax.random.fold_in(key_list[2], 1), NT // 16, (NT // 16 + NT // 64 + 2) - 1).astype(jnp.int32),
    }


def make_tables(count_time, count_freq):
    moments = jnp.arange(count_time, dtype=jnp.int32)
    frequency_bins = 1 + jnp.arange(count_freq, dtype=jnp.int32) * (count_time // (2 * count_freq))
    phase = (frequency_bins[:, None] * moments[None, :] % count_time).astype(jnp.float32) * (2.0 * math.pi / count_time)
    cosine = jnp.cos(phase)
    sine_part = jnp.sin(phase)
    stacked = jnp.concatenate([cosine, -sine_part], 0)
    forward_table = (stacked * count_time ** (-0.5)).astype(jnp.bfloat16)
    inverse_table = (stacked.T * math.sqrt(2.0 / count_freq)).astype(jnp.bfloat16)
    return (forward_table, inverse_table)

def reference(reflection, direct_focus, onset):
    forward_table, inverse_table = make_tables(NT, NF)
    moments = jnp.arange(NT, dtype=jnp.int32)
    signed_time = jnp.where(moments < NT // 2, moments, moments - NT)
    window = jnp.abs(signed_time)[None, :, None] < onset[:, None, :]

    def to_spectrum(field):
        spectrum = jnp.einsum('kt,ftr->fkr', forward_table.astype(jnp.float32), field.astype(jnp.float32))
        return spectrum.reshape(FOC, 2, NF, ORDER).astype(jnp.bfloat16)

    def to_time(values):
        flat = values.reshape(FOC, 2 * NF, ORDER).astype(jnp.float32)
        return jnp.einsum('tk,fkr->ftr', inverse_table.astype(jnp.float32), flat)

    def apply_reflection(spectrum, orient):
        by_freq = jnp.moveaxis(spectrum, 2, 0)

        def single(pair):
            matrix, spec_one = pair
            parts = jnp.einsum('ars,fbs->fabr', matrix.astype(jnp.float32), spec_one.astype(jnp.float32))
            real_part = parts[:, 0, 0] - orient * parts[:, 1, 1]
            imag_part = parts[:, 0, 1] + orient * parts[:, 1, 0]
            return jnp.stack([real_part, imag_part], 1)
        result = lax.map(single, (reflection, by_freq))
        return jnp.moveaxis(result, 0, 2).astype(jnp.bfloat16)
    focus = direct_focus
    for repeat in range(ITERS):
        values = apply_reflection(to_spectrum(focus), 1.0)
        upgoing = jnp.where(window, to_time(values), 0.0).astype(jnp.bfloat16)
        values = apply_reflection(to_spectrum(upgoing), -1.0)
        focus = (direct_focus.astype(jnp.float32) - jnp.where(window, to_time(values), 0.0)).astype(jnp.bfloat16)
    return focus
```

```python
import functools
import math

import jax
import jax.numpy as jnp
import ml_dtypes
import numpy as np
from jax import lax
from jax.experimental import pallas as pl
from jax.experimental.pallas import tpu as pltpu
from jax.sharding import Mesh
from jax.sharding import PartitionSpec as P

ITERS = 3
INNER = 64
OUTER = 80
EDGES = 2 * (OUTER - INNER + 1)
HEAD = 96
TAIL = 80
BF16 = ml_dtypes.bfloat16


def make_tables(count_time, count_freq):
    moments = np.arange(count_time)
    bins = 1 + np.arange(count_freq) * (count_time // (2 * count_freq))
    turns = bins[:, None] * moments[None, :] % count_time
    phase = turns.astype(np.float32) * np.float32(2.0 * math.pi / count_time)
    stacked = np.concatenate([np.cos(phase), -np.sin(phase)], 0).astype(np.float32)
    forward = (stacked * np.float32(count_time ** (-0.5))).astype(BF16)
    inverse = (stacked.T * np.float32(math.sqrt(2.0 / count_freq))).astype(BF16)
    return forward.astype(np.float64), inverse.astype(np.float64)


def spread(matrix, count):
    return np.kron(matrix, np.eye(count)).astype(BF16)


def make_constants(count_time, count_freq, groups, focal_local, sub):
    forward, inverse = make_tables(count_time, count_freq)
    local_freq = count_freq // groups
    order = np.array(
        [c * count_freq + g * local_freq + j for g in range(groups) for j in range(local_freq) for c in range(2)]
    )
    forward, inverse = forward[order], inverse[:, order]
    inside = np.array(list(range(INNER)) + list(range(count_time - INNER + 1, count_time)))
    edge = np.array(list(range(INNER, OUTER + 1)) + [count_time - s for s in range(INNER, OUTER + 1)])
    core = forward[:, inside] @ inverse[inside]
    high = core.astype(BF16).astype(np.float64)
    low = core - high
    per = 2 * local_freq
    to_edge = spread(inverse[edge], sub)
    mix, back = [], []
    for g in range(groups):
        rows = slice(g * per, (g + 1) * per)
        mix.append(np.concatenate([spread(high[rows], sub), spread(low[rows], sub)], 0))
        back.append(spread(forward[rows][:, edge], sub))
    first = np.einsum("kt,fg->kfgt", forward, np.eye(focal_local)).reshape(
        2 * count_freq * focal_local, focal_local * count_time
    )
    window_rows = np.array(list(range(HEAD)) + list(range(count_time - TAIL, count_time)))
    last = np.einsum("tk,fg->ftkg", inverse[window_rows], np.eye(focal_local)).reshape(
        focal_local * (HEAD + TAIL), 2 * count_freq * focal_local
    )
    return to_edge, np.stack(mix), np.stack(back), first.astype(BF16), last.astype(BF16)


def product_kernel(orient, copies, core_ref, r_ref, own_ref, other_ref, out_ref, acc_ref):
    step = pl.program_id(0)
    local_freq, _, rows, _ = r_ref.shape
    wide = own_ref.shape[1] // local_freq

    @pl.when(step == 0)
    def _():
        acc_ref[...] = jnp.zeros_like(acc_ref)

    first = core_ref[0] == 0
    own, other = own_ref[0], other_ref[0]
    x = jnp.concatenate([jnp.where(first, own, other), jnp.where(first, other, own)], axis=1)
    for j in range(local_freq):
        matrix = r_ref[j].reshape(2 * rows, r_ref.shape[3])
        acc_ref[j] += lax.dot_general(
            x[j * wide : (j + 1) * wide],
            matrix,
            (((1,), (1,)), ((), ())),
            preferred_element_type=jnp.float32,
        )

    @pl.when(step == pl.num_programs(0) - 1)
    def _():
        half = wide // 2
        for j in range(local_freq):
            real = acc_ref[j, :half, :rows] - orient * acc_ref[j, half:, rows:]
            imag = acc_ref[j, half:, :rows] + orient * acc_ref[j, :half, rows:]
            both = jnp.concatenate([real, imag], 0).astype(jnp.bfloat16)
            for d in range(copies):
                out_ref[d, j * wide : (j + 1) * wide] = both


def product(reflection, own, other, core, orient, copies):
    local_freq, _, rows, order = reflection.shape
    blocks, wide, _ = own.shape
    return pl.pallas_call(
        functools.partial(product_kernel, orient, copies),
        out_shape=jax.ShapeDtypeStruct((copies, wide, rows), jnp.bfloat16),
        grid_spec=pltpu.PrefetchScalarGridSpec(
            num_scalar_prefetch=1,
            grid=(blocks,),
            in_specs=[
                pl.BlockSpec((local_freq, 2, rows, order // blocks), lambda k, c: (0, 0, 0, k)),
                pl.BlockSpec((1, wide, rows), lambda k, c: (k, 0, 0)),
                pl.BlockSpec((1, wide, rows), lambda k, c: (k, 0, 0)),
            ],
            out_specs=pl.BlockSpec((copies, wide, rows), lambda k, c: (0, 0, 0)),
            scratch_shapes=[pltpu.VMEM((local_freq, wide // local_freq, 2 * rows), jnp.float32)],
        ),
        compiler_params=pltpu.CompilerParams(
            dimension_semantics=("arbitrary",), vmem_limit_bytes=24 << 20
        ),
        cost_estimate=pl.CostEstimate(
            flops=4 * reflection.size * wide // local_freq,
            bytes_accessed=2 * reflection.size,
            transcendentals=0,
        ),
    )(core, reflection, own, other)


def mixing_kernel(subtract, copies, v_ref, edge_ref, mix_ref, back_ref, onset_ref, start_ref, out_ref):
    total, focal, rows = v_ref.shape
    per = start_ref.shape[0]
    sub = edge_ref.shape[1] // total
    wide = per * sub
    for g in range(focal // sub):
        part = slice(g * sub, (g + 1) * sub)
        v = v_ref[:, part, :].reshape(total * sub, rows)
        at_edge = jnp.dot(edge_ref[...], v, preferred_element_type=jnp.float32)
        at_edge = at_edge.reshape(EDGES, sub, rows)
        number = lax.broadcasted_iota(jnp.int32, (EDGES, sub, rows), 0)
        time = INNER + jnp.where(number < EDGES // 2, number, number - EDGES // 2)
        kept = jnp.where(time < onset_ref[part, :][None], at_edge, 0.0).astype(jnp.bfloat16)
        both = jnp.dot(mix_ref[...], v, preferred_element_type=jnp.float32)
        result = both[:wide] + both[wide:]
        result += jnp.dot(
            back_ref[...], kept.reshape(EDGES * sub, rows), preferred_element_type=jnp.float32
        )
        result = result.reshape(per, sub, rows)
        if subtract:
            result = start_ref[:, part, :].astype(jnp.float32) - result
        result = result.astype(jnp.bfloat16)
        for d in range(copies):
            out_ref[d, :, part, :] = result


def mixing(values, tables, onset, start, subtract, copies):
    per, focal, rows = start.shape
    return pl.pallas_call(
        functools.partial(mixing_kernel, subtract, copies),
        out_shape=jax.ShapeDtypeStruct((copies, per, focal, rows), jnp.bfloat16),
        compiler_params=pltpu.CompilerParams(vmem_limit_bytes=24 << 20),
    )(values.reshape(-1, focal, rows), *tables, onset, start)


def shards(reflection, direct_focus, onset):
    groups = lax.axis_size("freq")
    pairs = lax.axis_size("pair")
    local_freq = reflection.shape[0]
    per = 2 * local_freq
    focal_local, count_time, rows = direct_focus.shape
    focal = focal_local * groups
    sub = 16
    to_edge, mix, back, first, last = make_constants(
        count_time, local_freq * groups, groups, focal_local, sub
    )
    here = lax.axis_index("freq")
    tables = (
        jnp.asarray(to_edge),
        lax.dynamic_index_in_dim(jnp.asarray(mix), here, 0, keepdims=False),
        lax.dynamic_index_in_dim(jnp.asarray(back), here, 0, keepdims=False),
    )
    core = lax.axis_index("core").astype(jnp.int32).reshape(1)

    def over(axis, value):
        return lax.all_to_all(value, axis, split_axis=0, concat_axis=0, tiled=True)

    def swap(value):
        return lax.ppermute(value, "core", [(0, 1), (1, 0)])

    def apply_reflection(spread_spectrum, orient, copies):
        own = over("pair", spread_spectrum)
        return product(reflection, own, swap(own), core, orient, copies)

    spectrum = jnp.dot(
        jnp.asarray(first),
        direct_focus.reshape(focal_local * count_time, rows),
        preferred_element_type=jnp.float32,
    ).astype(jnp.bfloat16)
    spectrum = spectrum.reshape(groups, per, focal_local, rows)
    levels = jnp.broadcast_to(
        onset.astype(jnp.bfloat16)[None, None], (groups, 1, focal_local, rows)
    )
    sent = jnp.concatenate([spectrum, levels], 1).reshape(groups, (per + 1) * focal_local, rows)
    got = over("freq", sent).reshape(groups, per + 1, focal_local, rows)
    got = jnp.swapaxes(got, 0, 1).reshape(per + 1, focal, rows)
    start, all_onset = got[:per], got[per].astype(jnp.int32)

    moving = jnp.broadcast_to(start.reshape(1, per * focal, rows), (pairs, per * focal, rows))
    for repeat in range(ITERS):
        values = apply_reflection(moving, 1.0, groups)
        values = over("freq", values)
        moving = mixing(values, tables, all_onset, start, False, pairs)
        moving = moving.reshape(pairs, per * focal, rows)
        if repeat < ITERS - 1:
            values = apply_reflection(moving, -1.0, groups)
            values = over("freq", values)
            moving = mixing(values, tables, all_onset, start, True, pairs)
            moving = moving.reshape(pairs, per * focal, rows)
    values = apply_reflection(moving, -1.0, 1)
    values = values.reshape(per, groups, focal_local, rows)
    values = jnp.swapaxes(values, 0, 1).reshape(groups, per * focal_local, rows)
    values = over("freq", values).reshape(groups * per * focal_local, rows)
    change = jnp.dot(jnp.asarray(last), values, preferred_element_type=jnp.float32)
    change = change.reshape(focal_local, HEAD + TAIL, rows)
    number = jnp.arange(HEAD + TAIL)
    distance = jnp.where(number < HEAD, number, HEAD + TAIL - number)
    change = jnp.where(distance[None, :, None] < onset[:, None, :], change, 0.0)

    def finish(part, piece):
        return (part.astype(jnp.float32) - piece).astype(jnp.bfloat16)

    return jnp.concatenate(
        [
            finish(direct_focus[:, :HEAD], change[:, :HEAD]),
            direct_focus[:, HEAD : count_time - TAIL],
            finish(direct_focus[:, count_time - TAIL :], change[:, HEAD:]),
        ],
        1,
    )


def solution(mesh):
    groups, blocks = mesh.devices.shape
    split = Mesh(mesh.devices.reshape(groups, blocks // 2, 2), ("freq", "pair", "core"))
    rows = ("pair", "core")
    return jax.shard_map(
        shards,
        mesh=split,
        in_specs=(P("freq", None, rows, None), P("freq", None, rows), P("freq", rows)),
        out_specs=P("freq", None, rows),
        check_vma=False,
    )
```

```python
import functools
import math

import jax
import jax.numpy as jnp
import ml_dtypes
import numpy as np
from jax import lax
from jax.experimental import pallas as pl
from jax.experimental.pallas import tpu as pltpu
from jax.sharding import Mesh
from jax.sharding import PartitionSpec as P

ITERS = 3
INNER = 64
OUTER = 80
EDGES = 2 * (OUTER - INNER + 1)
HEAD = 96
TAIL = 80
BF16 = ml_dtypes.bfloat16


def make_tables(count_time, count_freq):
    moments = np.arange(count_time)
    bins = 1 + np.arange(count_freq) * (count_time // (2 * count_freq))
    turns = bins[:, None] * moments[None, :] % count_time
    phase = turns.astype(np.float32) * np.float32(2.0 * math.pi / count_time)
    stacked = np.concatenate([np.cos(phase), -np.sin(phase)], 0).astype(np.float32)
    forward = (stacked * np.float32(count_time ** (-0.5))).astype(BF16)
    inverse = (stacked.T * np.float32(math.sqrt(2.0 / count_freq))).astype(BF16)
    return forward.astype(np.float64), inverse.astype(np.float64)


def spread(matrix, count):
    return np.kron(matrix, np.eye(count)).astype(BF16)


def make_constants(count_time, count_freq, groups, sets, focal_local, sub):
    forward, inverse = make_tables(count_time, count_freq)
    local_freq = count_freq // groups
    order = np.array(
        [c * count_freq + g * local_freq + j for g in range(groups) for j in range(local_freq) for c in range(2)]
    )
    forward, inverse = forward[order], inverse[:, order]
    inside = np.array(list(range(INNER)) + list(range(count_time - INNER + 1, count_time)))
    edge = np.array(list(range(INNER, OUTER + 1)) + [count_time - s for s in range(INNER, OUTER + 1)])
    core = forward[:, inside] @ inverse[inside]
    high = core.astype(BF16).astype(np.float64)
    low = core - high
    per = 2 * count_freq // sets
    to_edge = spread(inverse[edge], sub)
    mix, back = [], []
    for g in range(sets):
        rows = slice(g * per, (g + 1) * per)
        mix.append(np.concatenate([spread(high[rows], sub), spread(low[rows], sub)], 0))
        back.append(spread(forward[rows][:, edge], sub))
    first = np.einsum("kt,fg->kfgt", forward, np.eye(focal_local)).reshape(
        2 * count_freq * focal_local, focal_local * count_time
    )
    window_rows = np.array(list(range(HEAD)) + list(range(count_time - TAIL, count_time)))
    last = np.einsum("tk,fg->ftkg", inverse[window_rows], np.eye(focal_local)).reshape(
        focal_local * (HEAD + TAIL), 2 * count_freq * focal_local
    )
    return to_edge, np.stack(mix), np.stack(back), first.astype(BF16), last.astype(BF16)


def opening_kernel(set_ref, first_ref, direct_ref, mix_ref, back_ref, out_ref, mix_out, back_out, first_in, direct_in, sems):
    focal_local, count_time, _ = direct_ref.shape
    here = set_ref[0]
    tables = [
        pltpu.make_async_copy(mix_ref.at[here], mix_out, sems.at[0]),
        pltpu.make_async_copy(back_ref.at[here], back_out, sems.at[1]),
    ]
    fetch = [pltpu.make_async_copy(first_ref, first_in, sems.at[2])]
    fetch += [
        pltpu.make_async_copy(direct_ref.at[f], direct_in.at[f], sems.at[3 + f])
        for f in range(focal_local)
    ]
    for copy in fetch + tables:
        copy.start()
    fetch[0].wait()
    total = jnp.zeros((first_in.shape[0], direct_in.shape[2]), jnp.float32)
    for f in range(focal_local):
        fetch[1 + f].wait()
        total += jnp.dot(
            first_in[:, f * count_time : (f + 1) * count_time],
            direct_in[f],
            preferred_element_type=jnp.float32,
        )
    groups, copies, chunk, _ = out_ref.shape
    for g in range(groups):
        piece = total[g * chunk : (g + 1) * chunk].astype(jnp.bfloat16)
        for d in range(copies):
            out_ref[g, d] = piece
    for copy in tables:
        copy.wait()


def opening(first, direct_focus, mix, back, here, groups, copies):
    focal_local, count_time, rows = direct_focus.shape
    shape = (groups, copies, first.shape[0] // groups, rows)
    whole = pl.BlockSpec(memory_space=pltpu.HBM)
    local = pl.BlockSpec(memory_space=pltpu.VMEM)
    return pl.pallas_call(
        opening_kernel,
        out_shape=[
            jax.ShapeDtypeStruct(shape, jnp.bfloat16),
            jax.ShapeDtypeStruct(mix.shape[1:], jnp.bfloat16),
            jax.ShapeDtypeStruct(back.shape[1:], jnp.bfloat16),
        ],
        in_specs=[pl.BlockSpec(memory_space=pltpu.SMEM)] + [whole] * 4,
        out_specs=[local] * 3,
        scratch_shapes=[
            pltpu.VMEM(first.shape, jnp.bfloat16),
            pltpu.VMEM(direct_focus.shape, jnp.bfloat16),
            pltpu.SemaphoreType.DMA((3 + focal_local,)),
        ],
        compiler_params=pltpu.CompilerParams(vmem_limit_bytes=60 << 20),
        cost_estimate=pl.CostEstimate(
            flops=2 * first.size * rows,
            bytes_accessed=2 * (direct_focus.size + first.size),
            transcendentals=0,
        ),
    )(here, first, direct_focus, mix, back)


def part_of(ref, pairs, halves, first, j, p):
    count, wide, _ = ref.shape
    outer = count // pairs
    size = wide // 2
    pieces = [ref[o * pairs + p, j * size : (j + 1) * size] for o in range(outer)]
    return jnp.concatenate(pieces, 0)


def partial_product(r_ref, x_ref, core, steps, pairs, halves, first, j, total):
    rows = x_ref.shape[2]
    for p in steps:
        matrix, x = [], []
        for q in (p, p + 1):
            column = pl.multiple_of((2 * q + core) * rows, 128)
            matrix.append(r_ref[j, :, :, pl.ds(column, rows)].reshape(2 * rows, rows))
            x.append(part_of(x_ref, pairs, halves, first, j, q))
        total += lax.dot_general(
            jnp.concatenate(matrix, 1),
            jnp.concatenate(x, 1),
            (((1,), (1,)), ((), ())),
            preferred_element_type=jnp.float32,
        )
    return total


def own_kernel(pairs, halves, first, core_ref, r_ref, x_ref, sum_ref):
    for j in range(sum_ref.shape[0]):
        zero = jnp.zeros(sum_ref.shape[1:], jnp.float32)
        sum_ref[j] = partial_product(
            r_ref, x_ref, core_ref[0], range(0, pairs, 2), pairs, halves, first, j, zero
        )


def fetch_kernel(pairs, halves, core_ref, r_ref, x_ref, sum_ref, out_ref, sems):
    count = sems.shape[0]
    wide = r_ref.shape[3] // count
    copies = [
        pltpu.make_async_copy(
            r_ref.at[:, :, :, n * wide : (n + 1) * wide],
            out_ref.at[:, :, :, n * wide : (n + 1) * wide],
            sems.at[n],
        )
        for n in range(count)
    ]
    for copy in copies:
        copy.start()
    sum_ref[...] = jnp.zeros_like(sum_ref)
    step = pairs // count
    for n in range(count):
        copies[n].wait()
        for j in range(sum_ref.shape[0]):
            sum_ref[j] = partial_product(
                out_ref, x_ref, core_ref[0], range(n * step, (n + 1) * step, 2), pairs, halves, True, j, sum_ref[j]
            )


def other_kernel(pairs, halves, sets, orient, kind, *refs):
    core_ref, r_ref, x_ref, sum_ref, extra_ref, out_ref = refs[:6]
    first = kind == "first"
    rows = x_ref.shape[2]
    local_freq, _, columns = sum_ref.shape
    part = columns // halves
    sub = part // 2
    few = sub // sets
    for j in range(local_freq):
        total = partial_product(
            r_ref, x_ref, 1 - core_ref[0], range(0, pairs, 2), pairs, halves, first, j, sum_ref[j]
        )
        turned = total.T
        if first:
            turned = jnp.concatenate(
                [
                    turned[((x * halves + h) * 2 + c) * few : ((x * halves + h) * 2 + c + 1) * few]
                    for h in range(halves)
                    for c in range(2)
                    for x in range(sets)
                ],
                0,
            )
        for h in range(halves):
            real_in = turned[h * part : h * part + sub]
            imag_in = turned[h * part + sub : (h + 1) * part]
            real = real_in[:, :rows] - orient * imag_in[:, rows:]
            imag = imag_in[:, :rows] + orient * real_in[:, rows:]
            if kind == "last":
                for d in range(sets):
                    piece = slice(d * few, (d + 1) * few)
                    both = jnp.concatenate([real[piece], imag[piece]], 0).astype(jnp.bfloat16)
                    out_ref[d * halves + h, j * 2 * few : (j + 1) * 2 * few] = both
                continue
            both = jnp.concatenate([real, imag], 0)
            if first:
                refs[6][j, h] = both
            if kind == "update":
                both = extra_ref[j, h] - both
            both = both.astype(jnp.bfloat16)
            for d in range(sets):
                out_ref[d * halves + h, j * part : (j + 1) * part] = both
    if first:
        levels = extra_ref[...].astype(jnp.float32)
        levels = jnp.concatenate([levels, jnp.zeros_like(levels)], 0).astype(jnp.bfloat16)
        for d in range(out_ref.shape[0]):
            out_ref[d, local_freq * part :] = levels


def product(reflection, own, other, core, extra, orient, kind, sets, halves, pairs):
    local_freq, _, rows, _ = reflection.shape
    first = kind == "first"
    part = own.size // (local_freq * halves * pairs * rows)
    local = pl.BlockSpec(memory_space=pltpu.VMEM)
    small = pl.BlockSpec(memory_space=pltpu.SMEM)
    params = pltpu.CompilerParams(vmem_limit_bytes=8 << 20)
    cost = pl.CostEstimate(
        flops=reflection.size * halves * part, bytes_accessed=reflection.size, transcendentals=0
    )
    sums = jax.ShapeDtypeStruct((local_freq, 2 * rows, halves * part), jnp.float32)
    if first:
        half, reflection = pl.pallas_call(
            functools.partial(fetch_kernel, pairs, halves),
            out_shape=[sums, jax.ShapeDtypeStruct(reflection.shape, reflection.dtype)],
            in_specs=[small, pl.BlockSpec(memory_space=pl.ANY), local],
            out_specs=[local, local],
            scratch_shapes=[pltpu.SemaphoreType.DMA((pairs // 2,))],
            compiler_params=pltpu.CompilerParams(vmem_limit_bytes=28 << 20),
            cost_estimate=cost,
        )(core, reflection, own)
    else:
        half = pl.pallas_call(
            functools.partial(own_kernel, pairs, halves, False),
            out_shape=sums,
            in_specs=[small, local, local],
            out_specs=local,
            compiler_params=params,
            cost_estimate=cost,
        )(core, reflection, own)
    if kind == "last":
        height = local_freq * part // sets
    else:
        height = local_freq * part
    shapes = [(halves * sets, height, rows)]
    types = [jnp.bfloat16]
    if first:
        shapes = [(halves * sets, height + 2 * extra.shape[0], rows), (local_freq, halves, part, rows)]
        types.append(jnp.float32)
    values = pl.pallas_call(
        functools.partial(other_kernel, pairs, halves, sets, orient, kind),
        out_shape=[jax.ShapeDtypeStruct(shape, kept) for shape, kept in zip(shapes, types)],
        in_specs=[small, local, local, local, local],
        out_specs=[local] * len(shapes),
        compiler_params=params,
        cost_estimate=cost,
    )(core, reflection, other, half, extra)
    return (*values, reflection) if first else values


def mixing_kernel(copies, first, halves, half_ref, v_ref, edge_ref, mix_ref, back_ref, onset_ref, out_ref, *more):
    rows = v_ref.shape[2]
    wide = back_ref.shape[0]
    total = edge_ref.shape[1]
    sub = edge_ref.shape[0] // EDGES
    if first:
        count = total // v_ref.shape[0]
        v = v_ref[:, :count].reshape(total, rows)
        few = (v_ref.shape[1] - count) // 2
        levels = [
            v_ref[x * halves + half_ref[0], count:].astype(jnp.float32)[:few]
            for x in range(v_ref.shape[0] // halves)
        ]
        level = jnp.concatenate(levels, 0).astype(jnp.int32)
        more[0][...] = level
    else:
        v = v_ref[...].reshape(total, rows)
        level = onset_ref[...]
    at_edge = jnp.dot(edge_ref[...], v, preferred_element_type=jnp.float32)
    at_edge = at_edge.reshape(EDGES, sub, rows)
    number = lax.broadcasted_iota(jnp.int32, (EDGES, sub, rows), 0)
    time = INNER + jnp.where(number < EDGES // 2, number, number - EDGES // 2)
    kept = jnp.where(time < level[None], at_edge, 0.0).astype(jnp.bfloat16)
    both = jnp.dot(mix_ref[...], v, preferred_element_type=jnp.float32)
    result = both[:wide] + both[wide:]
    result += jnp.dot(
        back_ref[...], kept.reshape(EDGES * sub, rows), preferred_element_type=jnp.float32
    )
    result = result.astype(jnp.bfloat16)
    for h in range(halves):
        piece = result[h * (wide // halves) : (h + 1) * (wide // halves)]
        for d in range(copies):
            out_ref[h * copies + d] = piece


def mixing(values, tables, half, onset, first, halves, copies):
    rows = values.shape[2]
    sub = tables[0].shape[0] // EDGES
    wide = tables[2].shape[0]
    local = pl.BlockSpec(memory_space=pltpu.VMEM)
    shapes = [jax.ShapeDtypeStruct((halves * copies, wide // halves, rows), jnp.bfloat16)]
    if first:
        shapes.append(jax.ShapeDtypeStruct((sub, rows), jnp.int32))
    return pl.pallas_call(
        functools.partial(mixing_kernel, copies, first, halves),
        out_shape=shapes,
        in_specs=[pl.BlockSpec(memory_space=pltpu.SMEM)] + [local] * 5,
        out_specs=[local] * len(shapes),
        compiler_params=pltpu.CompilerParams(vmem_limit_bytes=8 << 20),
        cost_estimate=pl.CostEstimate(
            flops=2 * tables[0].size * rows, bytes_accessed=4 * values.size, transcendentals=0
        ),
    )(half, values, *tables, onset)


def finish_kernel(values_ref, last_ref, onset_ref, direct_ref, out_ref):
    _, count_time, rows = direct_ref.shape
    change = jnp.dot(last_ref[...], values_ref[...], preferred_element_type=jnp.float32)
    number = lax.broadcasted_iota(jnp.int32, change.shape, 0)
    distance = jnp.where(number < HEAD, number, HEAD + TAIL - number)
    change = jnp.where(distance < onset_ref[0], change, 0.0)
    end = count_time - TAIL
    out_ref[0, :HEAD] = (direct_ref[0, :HEAD].astype(jnp.float32) - change[:HEAD]).astype(jnp.bfloat16)
    out_ref[0, HEAD:end] = direct_ref[0, HEAD:end]
    out_ref[0, end:] = (direct_ref[0, end:].astype(jnp.float32) - change[HEAD:]).astype(jnp.bfloat16)


def finish(values, last, onset, direct_focus):
    focal_local, count_time, rows = direct_focus.shape
    block = pl.BlockSpec((1, count_time, rows), lambda f: (f, 0, 0))
    return pl.pallas_call(
        finish_kernel,
        out_shape=jax.ShapeDtypeStruct(direct_focus.shape, jnp.bfloat16),
        grid=(focal_local,),
        in_specs=[
            pl.BlockSpec(values.shape, lambda f: (0, 0)),
            pl.BlockSpec((HEAD + TAIL, values.shape[0]), lambda f: (f, 0)),
            pl.BlockSpec((1, 1, rows), lambda f: (f, 0, 0)),
            block,
        ],
        out_specs=block,
        compiler_params=pltpu.CompilerParams(vmem_limit_bytes=12 << 20),
    )(values, last, onset.reshape(focal_local, 1, rows), direct_focus)


def shards(reflection, direct_focus, onset):
    sets = lax.axis_size("x")
    halves = lax.axis_size("h")
    groups = sets * halves
    pairs = lax.axis_size("pair")
    local_freq = reflection.shape[0]
    per = 2 * local_freq
    focal_local, count_time, rows = direct_focus.shape
    sub = focal_local * sets
    to_edge, mix, back, first, last = make_constants(
        count_time, local_freq * groups, groups, sets, focal_local, sub
    )
    here = lax.axis_index("x").astype(jnp.int32).reshape(1)
    core = lax.axis_index("core").astype(jnp.int32).reshape(1)
    half = lax.axis_index("h").astype(jnp.int32).reshape(1)

    def over(axis, value):
        return lax.all_to_all(value, axis, split_axis=0, concat_axis=0, tiled=True)

    def apply_reflection(reflection, own, extra, orient, kind):
        other = lax.ppermute(own, "core", [(0, 1), (1, 0)])
        return product(reflection, own, other, core, extra, orient, kind, sets, halves, pairs)

    none, blank = jnp.zeros((8, 128), jnp.float32), jnp.zeros((8, 128), jnp.int32)
    to_edge, direct, core, half, none, blank = lax.optimization_barrier(
        (jnp.asarray(to_edge), direct_focus, core, half, none, blank)
    )
    sent, mix, back = opening(
        jnp.asarray(first), direct, jnp.asarray(mix), jnp.asarray(back), here, groups, pairs
    )
    tables = (to_edge, mix, back)
    sent = sent.reshape(groups * pairs, per * focal_local, rows)
    own = over(("x", "h", "pair"), sent)
    values, start, reflection = apply_reflection(reflection, own, onset, 1.0, "first")
    moving, all_onset = mixing(over(("x", "h"), values), tables, half, blank, True, halves, pairs)
    for step in range(1, 2 * ITERS):
        own = over(("h", "pair"), moving)
        if step == 2 * ITERS - 1:
            (values,) = apply_reflection(reflection, own, none, -1.0, "last")
            values = over(("x", "h"), values)
            break
        if step % 2:
            (values,) = apply_reflection(reflection, own, none, -1.0, "plain")
        else:
            (values,) = apply_reflection(reflection, own, start, 1.0, "update")
        (moving,) = mixing(over(("x", "h"), values), tables, half, all_onset, False, halves, pairs)
    return finish(
        values.reshape(groups * per * focal_local, rows), jnp.asarray(last), onset, direct_focus
    )


def solution(mesh):
    groups, blocks = mesh.devices.shape
    split = Mesh(mesh.devices.reshape(groups // 2, 2, blocks // 2, 2), ("x", "h", "pair", "core"))
    freq, rows = ("x", "h"), ("pair", "core")
    return jax.shard_map(
        shards,
        mesh=split,
        in_specs=(P(freq, None, rows, None), P(freq, None, rows), P(freq, rows)),
        out_specs=P(freq, None, rows),
        check_vma=False,
    )
```

```python
import functools
import math

import jax
import jax.numpy as jnp
import ml_dtypes
import numpy as np
from jax import lax
from jax.experimental import pallas as pl
from jax.experimental.pallas import tpu as pltpu
from jax.sharding import Mesh
from jax.sharding import PartitionSpec as P

ITERS = 3
INNER = 64
OUTER = 80
EDGES = 2 * (OUTER - INNER + 1)
HEAD = 96
TAIL = 80
BF16 = ml_dtypes.bfloat16


def make_tables(count_time, count_freq):
    moments = np.arange(count_time)
    bins = 1 + np.arange(count_freq) * (count_time // (2 * count_freq))
    turns = bins[:, None] * moments[None, :] % count_time
    phase = turns.astype(np.float32) * np.float32(2.0 * math.pi / count_time)
    stacked = np.concatenate([np.cos(phase), -np.sin(phase)], 0).astype(np.float32)
    forward = (stacked * np.float32(count_time ** (-0.5))).astype(BF16)
    inverse = (stacked.T * np.float32(math.sqrt(2.0 / count_freq))).astype(BF16)
    return forward.astype(np.float64), inverse.astype(np.float64)


def spread(matrix, count):
    return np.kron(matrix, np.eye(count)).astype(BF16)


def make_constants(count_time, count_freq, groups, sets, focal_local, sub):
    forward, inverse = make_tables(count_time, count_freq)
    local_freq = count_freq // groups
    order = np.array(
        [c * count_freq + g * local_freq + j for g in range(groups) for j in range(local_freq) for c in range(2)]
    )
    forward, inverse = forward[order], inverse[:, order]
    inside = np.array(list(range(INNER)) + list(range(count_time - INNER + 1, count_time)))
    edge = np.array(list(range(INNER, OUTER + 1)) + [count_time - s for s in range(INNER, OUTER + 1)])
    core = forward[:, inside] @ inverse[inside]
    high = core.astype(BF16).astype(np.float64)
    low = core - high
    per = 2 * count_freq // sets
    to_edge = spread(inverse[edge], sub)
    mix, back = [], []
    for g in range(sets):
        rows = slice(g * per, (g + 1) * per)
        mix.append(np.concatenate([spread(high[rows], sub), spread(low[rows], sub)], 0))
        back.append(spread(forward[rows][:, edge], sub))
    first = np.einsum("kt,fg->kfgt", forward, np.eye(focal_local)).reshape(
        2 * count_freq * focal_local, focal_local * count_time
    )
    window_rows = np.array(list(range(HEAD)) + list(range(count_time - TAIL, count_time)))
    last = np.einsum("tk,fg->ftkg", inverse[window_rows], np.eye(focal_local)).reshape(
        focal_local * (HEAD + TAIL), 2 * count_freq * focal_local
    )
    return to_edge, np.stack(mix), np.stack(back), first.astype(BF16), last.astype(BF16)


def opening_kernel(set_ref, first_ref, direct_ref, mix_ref, back_ref, out_ref, mix_out, back_out, first_in, direct_in, sems):
    focal_local, count_time, _ = direct_ref.shape
    here = set_ref[0]
    tables = [
        pltpu.make_async_copy(mix_ref.at[here], mix_out, sems.at[0]),
        pltpu.make_async_copy(back_ref.at[here], back_out, sems.at[1]),
    ]
    fetch = [pltpu.make_async_copy(first_ref, first_in, sems.at[2])]
    fetch += [
        pltpu.make_async_copy(direct_ref.at[f], direct_in.at[f], sems.at[3 + f])
        for f in range(focal_local)
    ]
    for copy in fetch + tables:
        copy.start()
    fetch[0].wait()
    total = jnp.zeros((first_in.shape[0], direct_in.shape[2]), jnp.float32)
    for f in range(focal_local):
        fetch[1 + f].wait()
        total += jnp.dot(
            first_in[:, f * count_time : (f + 1) * count_time],
            direct_in[f],
            preferred_element_type=jnp.float32,
        )
    out_ref[...] = total.astype(jnp.bfloat16)
    for copy in tables:
        copy.wait()


def spread_kernel(value_ref, out_ref):
    groups, copies, chunk, _ = out_ref.shape
    for g in range(groups):
        for d in range(copies):
            out_ref[g, d] = value_ref[g * chunk : (g + 1) * chunk]


def spread_out(value, groups, copies):
    shape = (groups, copies, value.shape[0] // groups, value.shape[1])
    return pl.pallas_call(
        spread_kernel,
        out_shape=jax.ShapeDtypeStruct(shape, value.dtype),
        in_specs=[pl.BlockSpec(memory_space=pltpu.VMEM)],
        out_specs=pl.BlockSpec(memory_space=pltpu.VMEM),
        compiler_params=pltpu.CompilerParams(vmem_limit_bytes=8 << 20),
        cost_estimate=pl.CostEstimate(flops=20000000000, bytes_accessed=60000000, transcendentals=0),
    )(value)


def opening(first, direct_focus, mix, back, here):
    focal_local, count_time, rows = direct_focus.shape
    shape = (first.shape[0], rows)
    whole = pl.BlockSpec(memory_space=pltpu.HBM)
    local = pl.BlockSpec(memory_space=pltpu.VMEM)
    return pl.pallas_call(
        opening_kernel,
        out_shape=[
            jax.ShapeDtypeStruct(shape, jnp.bfloat16),
            jax.ShapeDtypeStruct(mix.shape[1:], jnp.bfloat16),
            jax.ShapeDtypeStruct(back.shape[1:], jnp.bfloat16),
        ],
        in_specs=[pl.BlockSpec(memory_space=pltpu.SMEM)] + [whole] * 4,
        out_specs=[local] * 3,
        scratch_shapes=[
            pltpu.VMEM(first.shape, jnp.bfloat16),
            pltpu.VMEM(direct_focus.shape, jnp.bfloat16),
            pltpu.SemaphoreType.DMA((3 + focal_local,)),
        ],
        compiler_params=pltpu.CompilerParams(vmem_limit_bytes=53 << 20),
        cost_estimate=pl.CostEstimate(
            flops=2 * first.size * rows,
            bytes_accessed=2 * direct_focus.size,
            transcendentals=0,
        ),
    )(here, first, direct_focus, mix, back)


def part_of(ref, pairs, halves, first, j, p):
    count, wide, _ = ref.shape
    outer = count // pairs
    size = wide // 2
    pieces = [ref[o * pairs + p, j * size : (j + 1) * size] for o in range(outer)]
    return jnp.concatenate(pieces, 0)


def partial_product(r_ref, x_ref, core, pairs, halves, first, j, total):
    rows = x_ref.shape[2]
    for p in range(0, pairs, 2):
        matrix, x = [], []
        for q in (p, p + 1):
            column = pl.multiple_of((2 * q + core) * rows, 128)
            matrix.append(r_ref[j, :, :, pl.ds(column, rows)].reshape(2 * rows, rows))
            x.append(part_of(x_ref, pairs, halves, first, j, q))
        total += lax.dot_general(
            jnp.concatenate(matrix, 1),
            jnp.concatenate(x, 1),
            (((1,), (1,)), ((), ())),
            preferred_element_type=jnp.float32,
        )
    return total


def own_kernel(pairs, halves, first, core_ref, r_ref, x_ref, sum_ref):
    for j in range(sum_ref.shape[0]):
        zero = jnp.zeros(sum_ref.shape[1:], jnp.float32)
        sum_ref[j] = partial_product(r_ref, x_ref, core_ref[0], pairs, halves, first, j, zero)


def other_kernel(pairs, halves, sets, orient, kind, *refs):
    core_ref, r_ref, x_ref, sum_ref, extra_ref, out_ref = refs[:6]
    first = kind == "first"
    rows = x_ref.shape[2]
    local_freq, _, columns = sum_ref.shape
    part = columns // halves
    sub = part // 2
    few = sub // sets
    for j in range(local_freq):
        total = partial_product(
            r_ref, x_ref, 1 - core_ref[0], pairs, halves, first, j, sum_ref[j]
        )
        turned = total.T
        if first:
            turned = jnp.concatenate(
                [
                    turned[((x * halves + h) * 2 + c) * few : ((x * halves + h) * 2 + c + 1) * few]
                    for h in range(halves)
                    for c in range(2)
                    for x in range(sets)
                ],
                0,
            )
        for h in range(halves):
            real_in = turned[h * part : h * part + sub]
            imag_in = turned[h * part + sub : (h + 1) * part]
            real = real_in[:, :rows] - orient * imag_in[:, rows:]
            imag = imag_in[:, :rows] + orient * real_in[:, rows:]
            if kind == "last":
                for d in range(sets):
                    piece = slice(d * few, (d + 1) * few)
                    both = jnp.concatenate([real[piece], imag[piece]], 0).astype(jnp.bfloat16)
                    out_ref[d * halves + h, j * 2 * few : (j + 1) * 2 * few] = both
                continue
            both = jnp.concatenate([real, imag], 0)
            if first:
                refs[6][j, h] = both
            if kind == "update":
                both = extra_ref[j, h] - both
            both = both.astype(jnp.bfloat16)
            for d in range(sets):
                out_ref[d * halves + h, j * part : (j + 1) * part] = both
    if first:
        levels = extra_ref[...].astype(jnp.float32)
        levels = jnp.concatenate([levels, jnp.zeros_like(levels)], 0).astype(jnp.bfloat16)
        for d in range(out_ref.shape[0]):
            out_ref[d, local_freq * part :] = levels


def product(reflection, own, other, core, extra, orient, kind, sets, halves, pairs):
    local_freq, _, rows, _ = reflection.shape
    first = kind == "first"
    part = own.size // (local_freq * halves * pairs * rows)
    local = pl.BlockSpec(memory_space=pltpu.VMEM)
    small = pl.BlockSpec(memory_space=pltpu.SMEM)
    params = pltpu.CompilerParams(vmem_limit_bytes=8 << 20)
    cost = pl.CostEstimate(
        flops=reflection.size * halves * part, bytes_accessed=reflection.size, transcendentals=0
    )
    half = pl.pallas_call(
        functools.partial(own_kernel, pairs, halves, first),
        out_shape=jax.ShapeDtypeStruct((local_freq, 2 * rows, halves * part), jnp.float32),
        in_specs=[small, local, local],
        out_specs=local,
        compiler_params=params,
        cost_estimate=cost,
    )(core, reflection, own)
    if kind == "last":
        height = local_freq * part // sets
    else:
        height = local_freq * part
    shapes = [(halves * sets, height, rows)]
    types = [jnp.bfloat16]
    if first:
        shapes = [(halves * sets, height + 2 * extra.shape[0], rows), (local_freq, halves, part, rows)]
        types.append(jnp.float32)
    return pl.pallas_call(
        functools.partial(other_kernel, pairs, halves, sets, orient, kind),
        out_shape=[jax.ShapeDtypeStruct(shape, kept) for shape, kept in zip(shapes, types)],
        in_specs=[small, local, local, local, local],
        out_specs=[local] * len(shapes),
        compiler_params=params,
        cost_estimate=cost,
    )(core, reflection, other, half, extra)


def mixing_kernel(copies, first, halves, half_ref, v_ref, edge_ref, mix_ref, back_ref, onset_ref, out_ref, *more):
    rows = v_ref.shape[2]
    wide = back_ref.shape[0]
    total = edge_ref.shape[1]
    sub = edge_ref.shape[0] // EDGES
    if first:
        count = total // v_ref.shape[0]
        v = v_ref[:, :count].reshape(total, rows)
        few = (v_ref.shape[1] - count) // 2
        levels = [
            v_ref[x * halves + half_ref[0], count:].astype(jnp.float32)[:few]
            for x in range(v_ref.shape[0] // halves)
        ]
        level = jnp.concatenate(levels, 0).astype(jnp.int32)
        more[0][...] = level
    else:
        v = v_ref[...].reshape(total, rows)
        level = onset_ref[...]
    at_edge = jnp.dot(edge_ref[...], v, preferred_element_type=jnp.float32)
    at_edge = at_edge.reshape(EDGES, sub, rows)
    number = lax.broadcasted_iota(jnp.int32, (EDGES, sub, rows), 0)
    time = INNER + jnp.where(number < EDGES // 2, number, number - EDGES // 2)
    kept = jnp.where(time < level[None], at_edge, 0.0).astype(jnp.bfloat16)
    both = jnp.dot(mix_ref[...], v, preferred_element_type=jnp.float32)
    result = both[:wide] + both[wide:]
    result += jnp.dot(
        back_ref[...], kept.reshape(EDGES * sub, rows), preferred_element_type=jnp.float32
    )
    result = result.astype(jnp.bfloat16)
    for h in range(halves):
        piece = result[h * (wide // halves) : (h + 1) * (wide // halves)]
        for d in range(copies):
            out_ref[h * copies + d] = piece


def mixing(values, tables, half, onset, first, halves, copies):
    rows = values.shape[2]
    sub = tables[0].shape[0] // EDGES
    wide = tables[2].shape[0]
    local = pl.BlockSpec(memory_space=pltpu.VMEM)
    shapes = [jax.ShapeDtypeStruct((halves * copies, wide // halves, rows), jnp.bfloat16)]
    if first:
        shapes.append(jax.ShapeDtypeStruct((sub, rows), jnp.int32))
    return pl.pallas_call(
        functools.partial(mixing_kernel, copies, first, halves),
        out_shape=shapes,
        in_specs=[pl.BlockSpec(memory_space=pltpu.SMEM)] + [local] * 5,
        out_specs=[local] * len(shapes),
        compiler_params=pltpu.CompilerParams(vmem_limit_bytes=8 << 20),
        cost_estimate=pl.CostEstimate(
            flops=2 * tables[0].size * rows, bytes_accessed=4 * values.size, transcendentals=0
        ),
    )(half, values, *tables, onset)


def finish_kernel(values_ref, last_ref, onset_ref, direct_ref, out_ref):
    _, count_time, rows = direct_ref.shape
    change = jnp.dot(last_ref[...], values_ref[...], preferred_element_type=jnp.float32)
    number = lax.broadcasted_iota(jnp.int32, change.shape, 0)
    distance = jnp.where(number < HEAD, number, HEAD + TAIL - number)
    change = jnp.where(distance < onset_ref[pl.ds(pl.program_id(0), 1), :], change, 0.0)
    end = count_time - TAIL
    out_ref[0, :HEAD] = (direct_ref[0, :HEAD].astype(jnp.float32) - change[:HEAD]).astype(jnp.bfloat16)
    out_ref[0, HEAD:end] = direct_ref[0, HEAD:end]
    out_ref[0, end:] = (direct_ref[0, end:].astype(jnp.float32) - change[HEAD:]).astype(jnp.bfloat16)


def finish(values, last, onset, direct_focus):
    focal_local, count_time, rows = direct_focus.shape
    block = pl.BlockSpec((1, count_time, rows), lambda f: (f, 0, 0))
    return pl.pallas_call(
        finish_kernel,
        out_shape=jax.ShapeDtypeStruct(direct_focus.shape, jnp.bfloat16),
        grid=(focal_local,),
        in_specs=[
            pl.BlockSpec(values.shape, lambda f: (0, 0)),
            pl.BlockSpec((HEAD + TAIL, values.shape[0]), lambda f: (f, 0)),
            pl.BlockSpec((focal_local, rows), lambda f: (0, 0)),
            block,
        ],
        out_specs=block,
        compiler_params=pltpu.CompilerParams(vmem_limit_bytes=12 << 20),
    )(values, last, onset, direct_focus)


def shards(reflection, direct_focus, onset):
    sets = lax.axis_size("x")
    halves = lax.axis_size("h")
    groups = sets * halves
    pairs = lax.axis_size("pair")
    local_freq = reflection.shape[0]
    per = 2 * local_freq
    focal_local, count_time, rows = direct_focus.shape
    sub = focal_local * sets
    to_edge, mix, back, first, last = make_constants(
        count_time, local_freq * groups, groups, sets, focal_local, sub
    )
    here = lax.axis_index("x").astype(jnp.int32).reshape(1)
    core = lax.axis_index("core").astype(jnp.int32).reshape(1)
    half = lax.axis_index("h").astype(jnp.int32).reshape(1)

    def over(axis, value):
        return lax.all_to_all(value, axis, split_axis=0, concat_axis=0, tiled=True)

    def apply_reflection(own, extra, orient, kind):
        other = lax.ppermute(own, "core", [(0, 1), (1, 0)])
        return product(reflection, own, other, core, extra, orient, kind, sets, halves, pairs)

    none, blank = jnp.zeros((8, 128), jnp.float32), jnp.zeros((8, 128), jnp.int32)
    to_edge, direct, core, half, none, blank = lax.optimization_barrier(
        (jnp.asarray(to_edge), direct_focus, core, half, none, blank)
    )
    sent, mix, back = opening(
        jnp.asarray(first), direct, jnp.asarray(mix), jnp.asarray(back), here
    )
    sent = spread_out(sent, groups, pairs)
    tables = (to_edge, mix, back)
    sent = sent.reshape(groups * pairs, per * focal_local, rows)
    own = over(("x", "h", "pair"), sent)
    values, start = apply_reflection(own, onset, 1.0, "first")
    moving, all_onset = mixing(over(("x", "h"), values), tables, half, blank, True, halves, pairs)
    for step in range(1, 2 * ITERS):
        own = over(("h", "pair"), moving)
        if step == 2 * ITERS - 1:
            (values,) = apply_reflection(own, none, -1.0, "last")
            values = over(("x", "h"), values)
            break
        if step % 2:
            (values,) = apply_reflection(own, none, -1.0, "plain")
        else:
            (values,) = apply_reflection(own, start, 1.0, "update")
        (moving,) = mixing(over(("x", "h"), values), tables, half, all_onset, False, halves, pairs)
    return finish(
        values.reshape(groups * per * focal_local, rows), jnp.asarray(last), onset, direct_focus
    )


def solution(mesh):
    groups, blocks = mesh.devices.shape
    split = Mesh(mesh.devices.reshape(groups // 2, 2, blocks // 2, 2), ("x", "h", "pair", "core"))
    freq, rows = ("x", "h"), ("pair", "core")
    return jax.shard_map(
        shards,
        mesh=split,
        in_specs=(P(freq, None, rows, None), P(freq, None, rows), P(freq, rows)),
        out_specs=P(freq, None, rows),
        check_vma=False,
    )
```

```python
import functools
import math

import jax
import jax.numpy as jnp
import ml_dtypes
import numpy as np
from jax import lax
from jax.experimental import pallas as pl
from jax.experimental.pallas import tpu as pltpu
from jax.sharding import Mesh
from jax.sharding import PartitionSpec as P

ITERS = 3
INNER = 64
OUTER = 80
EDGES = 2 * (OUTER - INNER + 1)
HEAD = 96
TAIL = 80
BF16 = ml_dtypes.bfloat16


def make_tables(count_time, count_freq):
    moments = np.arange(count_time)
    bins = 1 + np.arange(count_freq) * (count_time // (2 * count_freq))
    turns = bins[:, None] * moments[None, :] % count_time
    phase = turns.astype(np.float32) * np.float32(2.0 * math.pi / count_time)
    stacked = np.concatenate([np.cos(phase), -np.sin(phase)], 0).astype(np.float32)
    forward = (stacked * np.float32(count_time ** (-0.5))).astype(BF16)
    inverse = (stacked.T * np.float32(math.sqrt(2.0 / count_freq))).astype(BF16)
    return forward.astype(np.float64), inverse.astype(np.float64)


def spread(matrix, count):
    return np.kron(matrix, np.eye(count)).astype(BF16)


def make_constants(count_time, count_freq, groups, sets, focal_local, sub):
    forward, inverse = make_tables(count_time, count_freq)
    local_freq = count_freq // groups
    order = np.array(
        [c * count_freq + g * local_freq + j for g in range(groups) for j in range(local_freq) for c in range(2)]
    )
    forward, inverse = forward[order], inverse[:, order]
    inside = np.array(list(range(INNER)) + list(range(count_time - INNER + 1, count_time)))
    edge = np.array(list(range(INNER, OUTER + 1)) + [count_time - s for s in range(INNER, OUTER + 1)])
    core = forward[:, inside] @ inverse[inside]
    high = core.astype(BF16).astype(np.float64)
    low = core - high
    per = 2 * count_freq // sets
    to_edge = spread(inverse[edge], sub)
    mix, back = [], []
    for g in range(sets):
        rows = slice(g * per, (g + 1) * per)
        mix.append(np.concatenate([spread(high[rows], sub), spread(low[rows], sub)], 0))
        back.append(spread(forward[rows][:, edge], sub))
    first = np.einsum("kt,fg->kfgt", forward, np.eye(focal_local)).reshape(
        2 * count_freq * focal_local, focal_local * count_time
    )
    window_rows = np.array(list(range(HEAD)) + list(range(count_time - TAIL, count_time)))
    last = np.einsum("tk,fg->ftkg", inverse[window_rows], np.eye(focal_local)).reshape(
        focal_local * (HEAD + TAIL), 2 * count_freq * focal_local
    )
    return to_edge, np.stack(mix), np.stack(back), first.astype(BF16), last.astype(BF16)


def opening_kernel(set_ref, first_ref, direct_ref, mix_ref, back_ref, out_ref, mix_out, back_out, first_in, direct_in, sems):
    focal_local, count_time, _ = direct_ref.shape
    here = set_ref[0]
    tables = [
        pltpu.make_async_copy(mix_ref.at[here], mix_out, sems.at[0]),
        pltpu.make_async_copy(back_ref.at[here], back_out, sems.at[1]),
    ]
    fetch = [pltpu.make_async_copy(first_ref, first_in, sems.at[2])]
    fetch += [
        pltpu.make_async_copy(direct_ref.at[f], direct_in.at[f], sems.at[3 + f])
        for f in range(focal_local)
    ]
    for copy in fetch + tables:
        copy.start()
    fetch[0].wait()
    total = jnp.zeros((first_in.shape[0], direct_in.shape[2]), jnp.float32)
    for f in range(focal_local):
        fetch[1 + f].wait()
        total += jnp.dot(
            first_in[:, f * count_time : (f + 1) * count_time],
            direct_in[f],
            preferred_element_type=jnp.float32,
        )
    out_ref[...] = total.astype(jnp.bfloat16)
    for copy in tables:
        copy.wait()


def spread_kernel(value_ref, out_ref):
    groups, copies, chunk, _ = out_ref.shape
    for g in range(groups):
        for d in range(copies):
            out_ref[g, d] = value_ref[g * chunk : (g + 1) * chunk]


def spread_out(value, groups, copies):
    shape = (groups, copies, value.shape[0] // groups, value.shape[1])
    return pl.pallas_call(
        spread_kernel,
        out_shape=jax.ShapeDtypeStruct(shape, value.dtype),
        in_specs=[pl.BlockSpec(memory_space=pltpu.VMEM)],
        out_specs=pl.BlockSpec(memory_space=pltpu.VMEM),
        compiler_params=pltpu.CompilerParams(vmem_limit_bytes=8 << 20),
        cost_estimate=pl.CostEstimate(flops=20000000000, bytes_accessed=60000000, transcendentals=0),
    )(value)


def opening(first, direct_focus, mix, back, here):
    focal_local, count_time, rows = direct_focus.shape
    shape = (first.shape[0], rows)
    whole = pl.BlockSpec(memory_space=pltpu.HBM)
    local = pl.BlockSpec(memory_space=pltpu.VMEM)
    return pl.pallas_call(
        opening_kernel,
        out_shape=[
            jax.ShapeDtypeStruct(shape, jnp.bfloat16),
            jax.ShapeDtypeStruct(mix.shape[1:], jnp.bfloat16),
            jax.ShapeDtypeStruct(back.shape[1:], jnp.bfloat16),
        ],
        in_specs=[pl.BlockSpec(memory_space=pltpu.SMEM)] + [whole] * 4,
        out_specs=[local] * 3,
        scratch_shapes=[
            pltpu.VMEM(first.shape, jnp.bfloat16),
            pltpu.VMEM(direct_focus.shape, jnp.bfloat16),
            pltpu.SemaphoreType.DMA((3 + focal_local,)),
        ],
        compiler_params=pltpu.CompilerParams(vmem_limit_bytes=53 << 20),
        cost_estimate=pl.CostEstimate(
            flops=2 * first.size * rows,
            bytes_accessed=2 * direct_focus.size,
            transcendentals=0,
        ),
    )(here, first, direct_focus, mix, back)


def part_of(ref, pairs, halves, first, j, p):
    count, wide, _ = ref.shape
    outer = count // pairs
    size = wide // 2
    pieces = [ref[o * pairs + p, j * size : (j + 1) * size] for o in range(outer)]
    return jnp.concatenate(pieces, 0)


def partial_product(r_ref, x_ref, core, pairs, halves, first, j, total):
    rows = x_ref.shape[2]
    for p in range(0, pairs, 2):
        matrix, x = [], []
        for q in (p, p + 1):
            column = pl.multiple_of((2 * q + core) * rows, 128)
            matrix.append(r_ref[j, :, :, pl.ds(column, rows)].reshape(2 * rows, rows))
            x.append(part_of(x_ref, pairs, halves, first, j, q))
        total += lax.dot_general(
            jnp.concatenate(matrix, 1),
            jnp.concatenate(x, 1),
            (((1,), (1,)), ((), ())),
            preferred_element_type=jnp.float32,
        )
    return total


def own_kernel(pairs, halves, first, core_ref, r_ref, x_ref, sum_ref):
    for j in range(sum_ref.shape[0]):
        zero = jnp.zeros(sum_ref.shape[1:], jnp.float32)
        sum_ref[j] = partial_product(r_ref, x_ref, core_ref[0], pairs, halves, first, j, zero)


def other_kernel(pairs, halves, sets, orient, kind, *refs):
    core_ref, r_ref, x_ref, sum_ref, extra_ref, out_ref = refs[:6]
    first = kind == "first"
    rows = x_ref.shape[2]
    local_freq, _, columns = sum_ref.shape
    part = columns // halves
    sub = part // 2
    few = sub // sets
    for j in range(local_freq):
        total = partial_product(
            r_ref, x_ref, 1 - core_ref[0], pairs, halves, first, j, sum_ref[j]
        )
        turned = total.T
        if first:
            turned = jnp.concatenate(
                [
                    turned[((x * halves + h) * 2 + c) * few : ((x * halves + h) * 2 + c + 1) * few]
                    for h in range(halves)
                    for c in range(2)
                    for x in range(sets)
                ],
                0,
            )
        for h in range(halves):
            real_in = turned[h * part : h * part + sub]
            imag_in = turned[h * part + sub : (h + 1) * part]
            real = real_in[:, :rows] - orient * imag_in[:, rows:]
            imag = imag_in[:, :rows] + orient * real_in[:, rows:]
            if kind == "last":
                for d in range(sets):
                    piece = slice(d * few, (d + 1) * few)
                    both = jnp.concatenate([real[piece], imag[piece]], 0).astype(jnp.bfloat16)
                    out_ref[d * halves + h, j * 2 * few : (j + 1) * 2 * few] = both
                continue
            both = jnp.concatenate([real, imag], 0)
            if first:
                refs[6][j, h] = both
            if kind == "update":
                both = extra_ref[j, h] - both
            both = both.astype(jnp.bfloat16)
            for d in range(sets):
                out_ref[d * halves + h, j * part : (j + 1) * part] = both
    if first:
        levels = extra_ref[...].astype(jnp.float32)
        levels = jnp.concatenate([levels, jnp.zeros_like(levels)], 0).astype(jnp.bfloat16)
        for d in range(out_ref.shape[0]):
            out_ref[d, local_freq * part :] = levels


def product(reflection, own, other, core, extra, orient, kind, sets, halves, pairs):
    local_freq, _, rows, _ = reflection.shape
    first = kind == "first"
    part = own.size // (local_freq * halves * pairs * rows)
    local = pl.BlockSpec(memory_space=pltpu.VMEM)
    small = pl.BlockSpec(memory_space=pltpu.SMEM)
    params = pltpu.CompilerParams(vmem_limit_bytes=8 << 20)
    cost = pl.CostEstimate(
        flops=reflection.size * halves * part, bytes_accessed=reflection.size, transcendentals=0
    )
    half = pl.pallas_call(
        functools.partial(own_kernel, pairs, halves, first),
        out_shape=jax.ShapeDtypeStruct((local_freq, 2 * rows, halves * part), jnp.float32),
        in_specs=[small, local, local],
        out_specs=local,
        compiler_params=params,
        cost_estimate=cost,
    )(core, reflection, own)
    if kind == "last":
        height = local_freq * part // sets
    else:
        height = local_freq * part
    shapes = [(halves * sets, height, rows)]
    types = [jnp.bfloat16]
    if first:
        shapes = [(halves * sets, height + 2 * extra.shape[0], rows), (local_freq, halves, part, rows)]
        types.append(jnp.float32)
    return pl.pallas_call(
        functools.partial(other_kernel, pairs, halves, sets, orient, kind),
        out_shape=[jax.ShapeDtypeStruct(shape, kept) for shape, kept in zip(shapes, types)],
        in_specs=[small, local, local, local, local],
        out_specs=[local] * len(shapes),
        compiler_params=params,
        cost_estimate=cost,
    )(core, reflection, other, half, extra)


def mixing_kernel(copies, first, halves, half_ref, v_ref, edge_ref, mix_ref, back_ref, onset_ref, out_ref, *more):
    rows = v_ref.shape[2]
    wide = back_ref.shape[0]
    total = edge_ref.shape[1]
    sub = edge_ref.shape[0] // EDGES
    if first:
        count = total // v_ref.shape[0]
        v = v_ref[:, :count].reshape(total, rows)
        few = (v_ref.shape[1] - count) // 2
        levels = [
            v_ref[x * halves + half_ref[0], count:].astype(jnp.float32)[:few]
            for x in range(v_ref.shape[0] // halves)
        ]
        level = jnp.concatenate(levels, 0).astype(jnp.int32)
        more[0][...] = level
    else:
        v = v_ref[...].reshape(total, rows)
        level = onset_ref[...]
    at_edge = jnp.dot(edge_ref[...], v, preferred_element_type=jnp.float32)
    at_edge = at_edge.reshape(EDGES, sub, rows)
    number = lax.broadcasted_iota(jnp.int32, (EDGES, sub, rows), 0)
    time = INNER + jnp.where(number < EDGES // 2, number, number - EDGES // 2)
    kept = jnp.where(time < level[None], at_edge, 0.0).astype(jnp.bfloat16)
    both = jnp.dot(mix_ref[...], v, preferred_element_type=jnp.float32)
    result = both[:wide] + both[wide:]
    result += jnp.dot(
        back_ref[...], kept.reshape(EDGES * sub, rows), preferred_element_type=jnp.float32
    )
    result = result.astype(jnp.bfloat16)
    for h in range(halves):
        piece = result[h * (wide // halves) : (h + 1) * (wide // halves)]
        for d in range(copies):
            out_ref[h * copies + d] = piece


def mixing(values, tables, half, onset, first, halves, copies):
    rows = values.shape[2]
    sub = tables[0].shape[0] // EDGES
    wide = tables[2].shape[0]
    local = pl.BlockSpec(memory_space=pltpu.VMEM)
    shapes = [jax.ShapeDtypeStruct((halves * copies, wide // halves, rows), jnp.bfloat16)]
    if first:
        shapes.append(jax.ShapeDtypeStruct((sub, rows), jnp.int32))
    return pl.pallas_call(
        functools.partial(mixing_kernel, copies, first, halves),
        out_shape=shapes,
        in_specs=[pl.BlockSpec(memory_space=pltpu.SMEM)] + [local] * 5,
        out_specs=[local] * len(shapes),
        compiler_params=pltpu.CompilerParams(vmem_limit_bytes=8 << 20),
        cost_estimate=pl.CostEstimate(
            flops=2 * tables[0].size * rows, bytes_accessed=4 * values.size, transcendentals=0
        ),
    )(half, values, *tables, onset)


def finish_kernel(values_ref, last_ref, onset_ref, direct_ref, out_ref, ends_ref, sems):
    focal_local, count_time, _ = direct_ref.shape
    end = count_time - TAIL
    count = HEAD + TAIL
    copies = [
        pltpu.make_async_copy(
            direct_ref.at[:, HEAD:end], out_ref.at[:, HEAD:end], sems.at[2 * focal_local]
        )
    ]
    copies[0].start()
    for f in range(focal_local):
        change = jnp.dot(
            last_ref[f * count : (f + 1) * count], values_ref[...], preferred_element_type=jnp.float32
        )
        number = lax.broadcasted_iota(jnp.int32, change.shape, 0)
        distance = jnp.where(number < HEAD, number, count - number)
        change = jnp.where(distance < onset_ref[f : f + 1, :], change, 0.0)
        head = direct_ref[f, :HEAD].astype(jnp.float32) - change[:HEAD]
        tail = direct_ref[f, end:].astype(jnp.float32) - change[HEAD:]
        ends_ref[f, :HEAD] = head.astype(jnp.bfloat16)
        ends_ref[f, HEAD:] = tail.astype(jnp.bfloat16)
        for n, (rows, place) in enumerate(
            ((slice(0, HEAD), slice(0, HEAD)), (slice(HEAD, count), slice(end, count_time)))
        ):
            copy = pltpu.make_async_copy(
                ends_ref.at[f, rows], out_ref.at[f, place], sems.at[2 * f + n]
            )
            copy.start()
            copies.append(copy)
    for copy in copies:
        copy.wait()


def finish(values, last, onset, direct_focus):
    focal_local, _, rows = direct_focus.shape
    local = pl.BlockSpec(memory_space=pltpu.VMEM)
    return pl.pallas_call(
        finish_kernel,
        out_shape=jax.ShapeDtypeStruct(direct_focus.shape, jnp.bfloat16),
        in_specs=[local] * 4,
        out_specs=pl.BlockSpec(memory_space=pltpu.HBM),
        scratch_shapes=[
            pltpu.VMEM((focal_local, HEAD + TAIL, rows), jnp.bfloat16),
            pltpu.SemaphoreType.DMA((2 * focal_local + 1,)),
        ],
        compiler_params=pltpu.CompilerParams(vmem_limit_bytes=8 << 20),
    )(values, last, onset, direct_focus)


def shards(reflection, direct_focus, onset):
    sets = lax.axis_size("x")
    halves = lax.axis_size("h")
    groups = sets * halves
    pairs = lax.axis_size("pair")
    local_freq = reflection.shape[0]
    per = 2 * local_freq
    focal_local, count_time, rows = direct_focus.shape
    sub = focal_local * sets
    to_edge, mix, back, first, last = make_constants(
        count_time, local_freq * groups, groups, sets, focal_local, sub
    )
    here = lax.axis_index("x").astype(jnp.int32).reshape(1)
    core = lax.axis_index("core").astype(jnp.int32).reshape(1)
    half = lax.axis_index("h").astype(jnp.int32).reshape(1)

    def over(axis, value):
        return lax.all_to_all(value, axis, split_axis=0, concat_axis=0, tiled=True)

    def apply_reflection(own, extra, orient, kind):
        other = lax.ppermute(own, "core", [(0, 1), (1, 0)])
        return product(reflection, own, other, core, extra, orient, kind, sets, halves, pairs)

    none, blank = jnp.zeros((8, 128), jnp.float32), jnp.zeros((8, 128), jnp.int32)
    to_edge, direct, core, half, none, blank = lax.optimization_barrier(
        (jnp.asarray(to_edge), direct_focus, core, half, none, blank)
    )
    sent, mix, back = opening(
        jnp.asarray(first), direct, jnp.asarray(mix), jnp.asarray(back), here
    )
    sent = spread_out(sent, groups, pairs)
    tables = (to_edge, mix, back)
    sent = sent.reshape(groups * pairs, per * focal_local, rows)
    own = over(("x", "h", "pair"), sent)
    values, start = apply_reflection(own, onset, 1.0, "first")
    moving, all_onset = mixing(over(("x", "h"), values), tables, half, blank, True, halves, pairs)
    for step in range(1, 2 * ITERS):
        own = over(("h", "pair"), moving)
        if step == 2 * ITERS - 1:
            (values,) = apply_reflection(own, none, -1.0, "last")
            values = over(("x", "h"), values)
            break
        if step % 2:
            (values,) = apply_reflection(own, none, -1.0, "plain")
        else:
            (values,) = apply_reflection(own, start, 1.0, "update")
        (moving,) = mixing(over(("x", "h"), values), tables, half, all_onset, False, halves, pairs)
    return finish(
        values.reshape(groups * per * focal_local, rows), jnp.asarray(last), onset, direct_focus
    )


def solution(mesh):
    groups, blocks = mesh.devices.shape
    split = Mesh(mesh.devices.reshape(groups // 2, 2, blocks // 2, 2), ("x", "h", "pair", "core"))
    freq, rows = ("x", "h"), ("pair", "core")
    return jax.shard_map(
        shards,
        mesh=split,
        in_specs=(P(freq, None, rows, None), P(freq, None, rows), P(freq, rows)),
        out_specs=P(freq, None, rows),
        check_vma=False,
    )
```
